32 devices in a mesh: row: 2 (over y), col: 4 (over x, core), frame: 4 (over z).
Axes of the slice: x: 2, y: 2, z: 4, core: 2. Of those that a mesh axis runs over, the one named last changes fastest.
Arguments:
- video: float32 [16, 576, 1024], P('frame', 'row', 'col'), may hold values from -60 to 60
- multiplier: float32 [16, 576, 1024], P('frame', 'row', 'col'), may hold values from -3 to 3
- foreground: float32 [16, 576, 1024], P('frame', 'row', 'col'), may hold values from -6 to 6
- basis: float32 [16, 576, 1024], P(None, 'row', 'col'), may hold values from -40 to 40
- coefficients: float32 [16, 16], P('frame'), may hold values from -10 to 10
Outputs:
- new_foreground: float32 [16, 576, 1024], P('frame', 'row', 'col')
- new_coefficients: float32 [16, 16], P('frame')
- new_basis: float32 [16, 576, 1024], P(None, ('row', 'frame'), 'col')
The draws below stay inside these ranges and needn't reach their ends.
All inputs are finite; a program needn't handle non-finite values.
Results may differ from the reference program's by a relative error of at most 0.0003.
Values sent between devices are 32-bit elements; how exact they have to be, the bound alone decides.
A program may use at most 128 MiB of HBM per device.

```python
import jax
import jax.numpy as jnp
from jax import lax

RANK = 16
PASSES = 3
FRAMES = 16
HEIGHT = 576
WIDTH = 1024


def factor_parts(key):
    folded = jax.random.fold_in(key, 101)
    streams = jax.random.split(folded, 6)
    rank_scale = jnp.exp(jax.random.uniform(streams[0], (RANK,), jnp.float32, -1.15, 1.15))
    rise_rows = 3.0 ** (jnp.arange(HEIGHT, dtype=jnp.float32) / HEIGHT - 0.5)
    rise_cols = 3.0 ** (jnp.arange(WIDTH, dtype=jnp.float32) / WIDTH - 0.5)
    pixel_scale = jnp.exp(jax.random.uniform(streams[1], (HEIGHT, WIDTH), jnp.float32, -1.15, 1.15)) * rise_rows[:, None] * rise_cols[None, :]
    shapes = jax.random.normal(streams[2], (RANK, HEIGHT, WIDTH), jnp.float32)
    true_basis = 0.5 * shapes * rank_scale[:, None, None] * pixel_scale[None, :, :]
    frame_scale = jnp.exp(jax.random.uniform(streams[4], (FRAMES,), jnp.float32, -1.15, 1.15)) * 3.0 ** (jnp.arange(FRAMES, dtype=jnp.float32) / FRAMES - 0.5)
    weights = jax.random.normal(streams[5], (FRAMES, RANK), jnp.float32)
    true_coeff = 0.25 * weights * frame_scale[:, None]
    return (true_basis, true_coeff)


def draw_video(key, part):
    true_basis, true_coeff = factor_parts(key)
    streams = jax.random.split(jax.random.fold_in(key, 202), 3)
    low_rank = jnp.einsum('fr,rhw->fhw', true_coeff, true_basis)
    spikes = 2.0 * jax.random.normal(streams[1], (FRAMES, HEIGHT, WIDTH), jnp.float32) * jax.random.bernoulli(streams[2], 0.1, (FRAMES, HEIGHT, WIDTH)).astype(jnp.float32)
    jitter = 0.3 * jax.random.normal(streams[0], (FRAMES, HEIGHT, WIDTH), jnp.float32)
    return jnp.clip(low_rank + jitter + spikes, -60.0, 60.0)


def draw_basis(key, part):
    true_basis, true_coeff = factor_parts(key)
    jitter = jax.random.normal(jax.random.fold_in(key, 303), (RANK, HEIGHT, WIDTH), jnp.float32)
    return jnp.clip(true_basis * (1.0 + 0.2 * jitter), -40.0, 40.0)


def draw_coefficients(key, part):
    true_basis, true_coeff = factor_parts(key)
    jitter = jax.random.normal(jax.random.fold_in(key, 404), (FRAMES, RANK), jnp.float32)
    return jnp.clip(true_coeff + 0.1 * jitter, -10.0, 10.0)


def block_scale(key, dims, pieces, least, top_value):
    level, own = 1.0, jax.random.fold_in(key, 6)
    for position, parts in pieces:
        draws = jnp.exp(jax.random.uniform(jax.random.fold_in(own, position), (parts,), jnp.float32, least / len(pieces), top_value / len(pieces)))
        level = level * jnp.repeat(draws, dims[position] // parts).reshape([-1 if axis == position else 1 for axis in range(len(dims))])
    return level


def centred(key, shape, scale, bound, cuts=(), kind=jnp.bfloat16):
    result = jax.random.normal(key, shape, jnp.float32) * scale
    if len(cuts) > 0:
        result = block_scale(key, shape, cuts, -0.22, 0.18) * result
    return jnp.clip(result, min=-bound, max=bound).astype(kind)


def setup_inputs(seed: int = 0) -> dict:
    arg_keys = jax.random.split(jax.random.key(seed), 6)
    video = draw_video(jax.random.fold_in(arg_keys[5], 71), 0)
    multiplier = centred(arg_keys[1], (FRAMES, HEIGHT, WIDTH), 0.5, 3.0, ((0, 4), (1, 2), (2, 4)), jnp.float32)
    foreground = centred(arg_keys[2], (FRAMES, HEIGHT, WIDTH), 1.0, 6.0, ((0, 4), (1, 2), (2, 4)), jnp.float32)
    basis = draw_basis(jax.random.fold_in(arg_keys[5], 71), 0)
    coefficients = draw_coefficients(jax.random.fold_in(arg_keys[5], 71), 0)
    return dict(video=video, multiplier=multiplier, foreground=foreground, basis=basis, coefficients=coefficients)


relax_rate = 0.8
smooth_weight = 0.5
smooth_floor = 0.25
shrink_level = 0.4
dual_scale = 0.8
ridge_share = 0.1

def forward_cells(padded, direction, shape):
    starts = [0, 0, 0]
    starts[direction] = 1
    limits = [starts[axis_dim] + shape[axis_dim] for axis_dim in range(3)]
    return lax.slice(padded, starts, limits)

def descend(padded, source, anchor, extent):
    shape = tuple((int(length) - 1 for length in padded.shape))
    here_cells = padded[:-1, :-1, :-1]
    slopes = []
    for direction in range(3):
        ahead_cells = forward_cells(padded, direction, shape)
        places = anchor[direction] + jnp.arange(shape[direction], dtype=jnp.int32)
        inside = (places >= 0) & (places < extent[direction] - 1)
        layout = [1, 1, 1]
        layout[direction] = shape[direction]
        inside = inside.reshape(layout)
        slopes.append(jnp.where(inside, ahead_cells - here_cells, jnp.zeros_like(here_cells)))
    weight = lax.rsqrt(smooth_floor + slopes[0] * slopes[0] + slopes[1] * slopes[1] + slopes[2] * slopes[2])
    fluxes = [slope_part * weight for slope_part in slopes]
    spread = fluxes[0][1:, 1:, 1:] - fluxes[0][:-1, 1:, 1:] + (fluxes[1][1:, 1:, 1:] - fluxes[1][1:, :-1, 1:]) + (fluxes[2][1:, 1:, 1:] - fluxes[2][1:, 1:, :-1])
    center = padded[1:-1, 1:-1, 1:-1]
    return center + relax_rate * (source - center + smooth_weight * spread)

def solve_definite(matrix, right_side):
    factor_lower = jnp.linalg.cholesky(matrix)
    half_solved = lax.linalg.triangular_solve(factor_lower, right_side, left_side=True, lower=True)
    return lax.linalg.triangular_solve(factor_lower, half_solved, left_side=True, lower=True, transpose_a=True)

def reference(video, multiplier, foreground, basis, coefficients):
    highest = lax.Precision.HIGHEST
    flat_basis = basis.reshape(RANK, HEIGHT * WIDTH)
    background = jnp.dot(coefficients, flat_basis, precision=highest).reshape(FRAMES, HEIGHT, WIDTH)
    target = video - background + dual_scale * multiplier
    current = foreground
    for sweep in range(PASSES):
        padded = jnp.pad(current, 1)
        current = descend(padded, target, (-1, -1, -1), (FRAMES, HEIGHT, WIDTH))
    shrunk = current - jnp.clip(current, -shrink_level, shrink_level)
    residual_target = video + dual_scale * multiplier - shrunk
    flat_target = residual_target.reshape(FRAMES, HEIGHT * WIDTH)
    gram_sum = jnp.dot(flat_basis, flat_basis.T, precision=highest)
    cross_sum = jnp.dot(flat_basis, flat_target.T, precision=highest)
    identity_matrix = jnp.eye(RANK, dtype=gram_sum.dtype)
    pixel_ridge = ridge_share * HEIGHT * WIDTH
    coeff_rows = solve_definite(gram_sum + pixel_ridge * identity_matrix, cross_sum + pixel_ridge * coefficients.T)
    frame_total = jnp.dot(coeff_rows, flat_target, precision=highest)
    frame_gram = jnp.dot(coeff_rows, coeff_rows.T, precision=highest)
    frame_ridge = ridge_share * FRAMES
    new_basis = solve_definite(frame_gram + frame_ridge * identity_matrix, frame_total + frame_ridge * flat_basis)
    return (shrunk, coeff_rows.T, new_basis.reshape(RANK, HEIGHT, WIDTH))
```

```python
import functools

import jax
import jax.numpy as jnp
from jax import lax
from jax.experimental import pallas as pl
from jax.experimental.pallas import tpu as pltpu
from jax.sharding import PartitionSpec as P

PASSES = 3


relax_rate = 0.8
smooth_weight = 0.5
smooth_floor = 0.25
shrink_level = 0.4
dual_scale = 0.8
ridge_share = 0.1


def with_halo(block, sides, width):
    for axis, dim in sides:
        count = lax.axis_size(axis)
        forward = [(i, i + 1) for i in range(count - 1)]
        backward = [(target, source) for source, target in forward]
        low = lax.ppermute(
            lax.slice_in_dim(block, block.shape[dim] - width, None, axis=dim), axis, forward
        )
        high = lax.ppermute(lax.slice_in_dim(block, 0, width, axis=dim), axis, backward)
        block = jnp.concatenate([low, block, high], axis=dim)
    return block


def forward_cells(padded, direction, shape):
    starts = [0, 0, 0]
    starts[direction] = 1
    limits = [starts[axis_dim] + shape[axis_dim] for axis_dim in range(3)]
    return lax.slice(padded, starts, limits)


def descend(padded, source, anchor, extent):
    shape = tuple((int(length) - 1 for length in padded.shape))
    here_cells = padded[:-1, :-1, :-1]
    slopes = []
    for direction in range(3):
        ahead_cells = forward_cells(padded, direction, shape)
        places = anchor[direction] + jnp.arange(shape[direction], dtype=jnp.int32)
        inside = (places >= 0) & (places < extent[direction] - 1)
        layout = [1, 1, 1]
        layout[direction] = shape[direction]
        inside = inside.reshape(layout)
        slopes.append(jnp.where(inside, ahead_cells - here_cells, jnp.zeros_like(here_cells)))
    weight = lax.rsqrt(
        smooth_floor + slopes[0] * slopes[0] + slopes[1] * slopes[1] + slopes[2] * slopes[2]
    )
    fluxes = [slope_part * weight for slope_part in slopes]
    spread = (
        fluxes[0][1:, 1:, 1:]
        - fluxes[0][:-1, 1:, 1:]
        + (fluxes[1][1:, 1:, 1:] - fluxes[1][1:, :-1, 1:])
        + (fluxes[2][1:, 1:, 1:] - fluxes[2][1:, 1:, :-1])
    )
    center = padded[1:-1, 1:-1, 1:-1]
    return center + relax_rate * (source - center + smooth_weight * spread)


def solve_definite(matrix, right_side):
    factor_lower = jnp.linalg.cholesky(matrix)
    half_solved = lax.linalg.triangular_solve(factor_lower, right_side, left_side=True, lower=True)
    return lax.linalg.triangular_solve(
        factor_lower, half_solved, left_side=True, lower=True, transpose_a=True
    )


def local(video, multiplier, foreground, basis, coefficients):
    highest = lax.Precision.HIGHEST
    frames_here, rows_here, cols_here = video.shape
    rank_size = basis.shape[0]
    frame_count = lax.axis_size("frame")
    row_count = lax.axis_size("row")
    col_count = lax.axis_size("col")
    extent = (frames_here * frame_count, rows_here * row_count, cols_here * col_count)
    frame_slot = lax.axis_index("frame")
    corner = (
        frame_slot * frames_here,
        lax.axis_index("row") * rows_here,
        lax.axis_index("col") * cols_here,
    )
    pixels = rows_here * cols_here
    flat_basis = basis.reshape(rank_size, pixels)
    background = jnp.dot(coefficients, flat_basis, precision=highest).reshape(video.shape)
    target = video - background + dual_scale * multiplier
    current = foreground
    for sweep in range(PASSES):
        padded = with_halo(current, (("row", 1), ("col", 2), ("frame", 0)), 1)
        current = descend(padded, target, tuple((start_cell - 1 for start_cell in corner)), extent)
    shrunk = current - jnp.clip(current, -shrink_level, shrink_level)
    residual_target = video + dual_scale * multiplier - shrunk
    flat_target = residual_target.reshape(frames_here, pixels)
    gram_part = jnp.dot(flat_basis, flat_basis.T, precision=highest)
    cross_part = jnp.dot(flat_basis, flat_target.T, precision=highest)
    gram_sum, cross_sum = lax.psum((gram_part, cross_part), ("row", "col"))
    identity_matrix = jnp.eye(rank_size, dtype=gram_sum.dtype)
    pixel_ridge = ridge_share * pixels * row_count * col_count
    coeff_rows = solve_definite(
        gram_sum + pixel_ridge * identity_matrix, cross_sum + pixel_ridge * coefficients.T
    )
    total_part = jnp.dot(coeff_rows, flat_target, precision=highest).reshape(
        rank_size, rows_here, cols_here
    )
    frame_gram_part = jnp.dot(coeff_rows, coeff_rows.T, precision=highest)
    owned_rows = rows_here // frame_count
    owned_sums = lax.psum_scatter(total_part, "frame", scatter_dimension=1, tiled=True)
    frame_gram = lax.psum(frame_gram_part, "frame")
    old_owned = lax.dynamic_slice_in_dim(basis, frame_slot * owned_rows, owned_rows, 1)
    frame_ridge = ridge_share * frames_here * frame_count
    right_side = (owned_sums + frame_ridge * old_owned).reshape(rank_size, owned_rows * cols_here)
    new_basis = solve_definite(frame_gram + frame_ridge * identity_matrix, right_side)
    return (shrunk, coeff_rows.T, new_basis.reshape(rank_size, owned_rows, cols_here))


MESH = pl.DeviceIdType.MESH
CHUNK = 32


def eliminate(matrix, size):
    lanes = lax.broadcasted_iota(jnp.int32, matrix.shape, 1)
    rows = lax.broadcasted_iota(jnp.int32, matrix.shape, 0)
    for k in range(size):
        pivot = matrix[k : k + 1, k : k + 1]
        scaled = matrix[k : k + 1, :] / pivot
        column = jnp.sum(jnp.where(lanes == k, matrix, 0.0), axis=1, keepdims=True)
        matrix = jnp.where(rows == k, scaled, matrix - column * scaled)
    return matrix


def kernel(
    sizes, coeff_ref, video_hbm, mult_hbm, fore_hbm, basis_hbm,
    shrunk_hbm, rows_out, new_basis_hbm,
    field, video, mult, basis, anchor, target, result, owned,
    packed, arrived, corner, edge_next, edge_flux, first_cols,
    sums, parts, shares, square, table, table_smem,
    in_sems, out_sems, halo_send, halo_recv, part_send, part_recv,
    share_send, share_recv, move_send, move_recv, small_sem, barrier_own,
):
    F, H, W, rank, nr, nc, nz = sizes
    r = lax.axis_index("row")
    c = lax.axis_index("col")
    z = lax.axis_index("frame")
    own = H // nz

    def inside(dr, dc, dz):
        ok = None
        for at, step, count in ((r, dr, nr), (c, dc, nc), (z, dz, nz)):
            if step != 0:
                test = (at + step >= 0) & (at + step < count)
                ok = test if ok is None else ok & test
        return ok

    loads = []
    for i, (src, dst) in enumerate(
        (
            (fore_hbm, field.at[0, 1 : F + 1, 8 : H + 8, :]),
            (basis_hbm, basis),
            (video_hbm, video),
            (mult_hbm, mult),
        )
    ):
        copy = pltpu.make_async_copy(src, dst, in_sems.at[i])
        copy.start()
        loads.append(copy)

    barrier = pltpu.get_barrier_semaphore()
    for d in range(1, nr * nc):
        other = lax.rem(r * nc + c + d, nr * nc)
        pl.semaphore_signal(
            barrier, inc=1, device_id=(other // nc, lax.rem(other, nc), z), device_id_type=MESH
        )
    for d in range(1, nz):
        pl.semaphore_signal(
            barrier, inc=1, device_id=(r, c, lax.rem(z + d, nz)), device_id_type=MESH
        )
    diagonals = ((1, 0, -1), (-1, 0, 1), (0, 1, -1), (0, -1, 1))
    for step in diagonals:
        @pl.when(inside(*step))
        def _(step=step):
            pl.semaphore_signal(
                barrier,
                inc=1,
                device_id=(r + step[0], c + step[1], z + step[2]),
                device_id_type=MESH,
            )
    expected = jnp.int32(nr * nc - 1 + nz - 1)
    for step in diagonals:
        expected = expected + inside(*step).astype(jnp.int32)
    pl.semaphore_wait(barrier, expected)

    lane_h = lax.broadcasted_iota(jnp.int32, (H, 128), 1)

    def pack_columns(k):
        for side in range(2):
            tile = jnp.zeros((H, 128), jnp.float32)
            for f in range(F):
                at = 0 if side == 0 else W - 1
                lanes = field[k, f + 1, 8 : H + 8, (at // 128) * 128 : (at // 128) * 128 + 128]
                column = lanes[:, at % 128 : at % 128 + 1]
                tile = jnp.where(lane_h == f, column, tile)
            if side == 0:
                first_cols[...] = tile
            packed[k, side] = tile.T[:8, :]

    def halo_list(k):
        fk = field.at[k]
        mid = slice(1, F + 1)
        return (
            (fk.at[F, 8 : H + 8, :], fk.at[0, 8 : H + 8, :], (0, 0, 1)),
            (fk.at[1, 8 : H + 8, :], fk.at[F + 1, 8 : H + 8, :], (0, 0, -1)),
            (packed.at[k, 0], arrived.at[k, 0], (0, -1, 0)),
            (packed.at[k, 1], arrived.at[k, 1], (0, 1, 0)),
            (packed.at[k, 0], arrived.at[k, 2], (0, -1, 1)),
            (packed.at[k, 1], arrived.at[k, 3], (0, 1, -1)),
            (fk.at[mid, H : H + 8, :], fk.at[mid, 0:8, :], (1, 0, 0)),
            (fk.at[mid, 8:16, :], fk.at[mid, H + 8 : H + 16, :], (-1, 0, 0)),
            (fk.at[F, 8:16, :], fk.at[0, H + 8 : H + 16, :], (-1, 0, 1)),
            (fk.at[1, H : H + 8, :], fk.at[F + 1, 0:8, :], (1, 0, -1)),
            (fk.at[mid, H : H + 8, 0:128], corner.at[k, 0], (1, -1, 0)),
            (fk.at[mid, 8:16, W - 128 : W], corner.at[k, 1], (-1, 1, 0)),
        )

    def halo_copy(k, i, src, dst, step):
        return pltpu.make_async_remote_copy(
            src_ref=src, dst_ref=dst,
            send_sem=halo_send.at[k, i], recv_sem=halo_recv.at[k, i],
            device_id=(r + step[0], c + step[1], z + step[2]), device_id_type=MESH,
        )

    def send_halos(k):
        for i, (src, dst, step) in enumerate(halo_list(k)):
            @pl.when(inside(*step))
            def _(i=i, src=src, dst=dst, step=step):
                halo_copy(k, i, src, dst, step).start()

    def wait_halos(k):
        for i, (src, dst, step) in enumerate(halo_list(k)):
            @pl.when(inside(*(-s for s in step)))
            def _(i=i, src=src, dst=dst, step=step):
                halo_copy(k, i, src, dst, step).wait_recv()

    def finish_sends(k):
        for i, (src, dst, step) in enumerate(halo_list(k)):
            @pl.when(inside(*step))
            def _(i=i, src=src, dst=dst, step=step):
                halo_copy(k, i, src, dst, step).wait_send()

    def prepare_columns(k):
        tall = jnp.concatenate([arrived[k, 0], jnp.zeros((120, H), jnp.float32)], axis=0).T
        edge = jnp.concatenate([arrived[k, 2], jnp.zeros((120, H), jnp.float32)], axis=0).T
        tile = jnp.where(lane_h == 0, edge[:, F - 1 : F], pltpu.roll(tall, 1, 1))
        edge_next[8 : H + 8, :] = tile
        lane8 = lax.broadcasted_iota(jnp.int32, (8, 128), 1)
        top = jnp.zeros((8, 128), jnp.float32)
        bottom = jnp.zeros((1, 128), jnp.float32)
        for f in range(F):
            top = jnp.where(lane8 == f + 1, corner[k, 0, f][:, 0:1], top)
            bottom = jnp.where(lane8[:1] == f, corner[k, 1, f][0:1, 127:128], bottom)
        edge_next[0:8, :] = top
        edge_next[H + 8 : H + 16, :] = jnp.zeros((8, 128), jnp.float32)
        here = jnp.concatenate([arrived[k, 1], jnp.zeros((120, H), jnp.float32)], axis=0).T
        edge = jnp.concatenate([arrived[k, 3], jnp.zeros((120, H), jnp.float32)], axis=0).T
        ahead = jnp.where(lane_h == F - 1, edge[:, 0:1], pltpu.roll(here, 127, 1))
        slope0 = jnp.where((lane_h == F - 1) & (z == nz - 1), 0.0, ahead - here)
        row_h = lax.broadcasted_iota(jnp.int32, (H, 128), 0)
        below = jnp.where(row_h == H - 1, bottom, pltpu.roll(here, H - 1, 0))
        slope1 = jnp.where((row_h == H - 1) & (r == nr - 1), 0.0, below - here)
        slope2 = first_cols[...] - here
        weight = lax.rsqrt(smooth_floor + slope0 * slope0 + slope1 * slope1 + slope2 * slope2)
        edge_flux[...] = jnp.where(c == 0, 0.0, slope2 * weight)

    def sweep(k, last):
        @pl.loop(0, H // CHUNK)
        def _(step):
            start = pl.multiple_of(step * CHUNK, 8)
            R = CHUNK
            lane_t = lax.broadcasted_iota(jnp.int32, (R + 8, 128), 1)
            row_t = lax.broadcasted_iota(jnp.int32, (R + 8, W), 0) + (r * H + start - 8)
            lane_w = lax.broadcasted_iota(jnp.int32, (R + 8, W), 1)
            blocked = (row_t < 0) | (row_t >= nr * H - 1)
            columns = edge_next[pl.ds(start, R + 8), :]
            fluxes_in = edge_flux[pl.ds(start, R), :]
            now = field[k, 0, pl.ds(start, R + 16), :]
            flux0_before = None
            for f in range(-1, F):
                after = field[k, f + 2, pl.ds(start, R + 16), :]
                here = now[: R + 8]
                below = pltpu.roll(now, R + 15, 0)[: R + 8]
                ahead = after[: R + 8]
                wall = columns[:, f + 1 : f + 2]
                beyond = jnp.where(c == nc - 1, here, jnp.broadcast_to(wall, here.shape))
                right = jnp.where(lane_w == W - 1, beyond, pltpu.roll(here, W - 1, 1))
                slope0 = ahead - here
                if f == F - 1:
                    slope0 = jnp.where(z == nz - 1, 0.0, slope0)
                slope1 = jnp.where(blocked, 0.0, below - here)
                slope2 = right - here
                weight = lax.rsqrt(
                    smooth_floor + slope0 * slope0 + slope1 * slope1 + slope2 * slope2
                )
                flux0 = (slope0 * weight)[8:]
                if f < 0:
                    flux0 = jnp.where(z == 0, 0.0, flux0)
                else:
                    flux1 = jnp.where(row_t < 0, 0.0, slope1 * weight)
                    flux2 = (slope2 * weight)[8:]
                    above = pltpu.roll(flux1, 1, 0)[8:]
                    left = jnp.where(
                        lane_w[8:] == 0,
                        jnp.broadcast_to(fluxes_in[:, f : f + 1], flux2.shape),
                        pltpu.roll(flux2, 1, 1),
                    )
                    spread = flux0 - flux0_before + (flux1[8:] - above) + (flux2 - left)
                    center = here[8:]
                    at = pl.ds(start, R)
                    value = center + relax_rate * (
                        target[f, at, :] - center + smooth_weight * spread
                    )
                    if last:
                        shrunk = value - jnp.clip(value, -shrink_level, shrink_level)
                        result[f, at, :] = shrunk
                        anchor[f, at, :] = anchor[f, at, :] - shrunk
                    else:
                        field[k + 1, f + 1, pl.ds(start + 8, R), :] = value
                flux0_before = flux0
                now = after

    def products(left_of, right_of, lefts, rights, store):
        zero = jnp.zeros((8, 128), jnp.float32)

        def body(step, totals):
            rows = pl.ds(pl.multiple_of(step * 8, 8), 8)
            a = [left_of[i, rows, :] for i in lefts]
            b = [right_of[j, rows, :] for j in rights]
            out = []
            for x in range(len(lefts)):
                for y in range(len(rights)):
                    prod = a[x] * b[y]
                    total = totals[len(out)]
                    for w in range(W // 128):
                        total = total + prod[:, w * 128 : w * 128 + 128]
                    out.append(total)
            return tuple(out)

        totals = lax.fori_loop(0, H // 8, body, (zero,) * (len(lefts) * len(rights)), unroll=2)
        n = 0
        for i in lefts:
            for j in rights:
                store(i, j, jnp.sum(totals[n], axis=0, keepdims=True))
                n += 1

    loads[0].wait()
    pack_columns(0)
    send_halos(0)
    loads[1].wait()

    def store_gram(i, j, value):
        sums[j, i : i + 1, :] = value
        if i // 4 != j // 4:
            sums[i, j : j + 1, :] = value

    for i in range(0, rank, 4):
        for j in range(i, rank, 4):
            products(basis, basis, range(i, i + 4), range(j, j + 4), store_gram)

    loads[2].wait()
    loads[3].wait()

    @pl.loop(0, H // 8)
    def _(step):
        rows = pl.ds(pl.multiple_of(step * 8, 8), 8)
        totals = [None] * F
        for q in range(rank):
            plane = basis[q, rows, :]
            for f in range(F):
                term = coeff_ref[f, q] * plane
                totals[f] = term if totals[f] is None else totals[f] + term
        for f in range(F):
            lifted = dual_scale * mult[f, rows, :]
            anchor[f, rows, :] = video[f, rows, :] + lifted
            target[f, rows, :] = video[f, rows, :] - totals[f] + lifted

    for k in range(PASSES):
        wait_halos(k)
        prepare_columns(k)
        sweep(k, k == PASSES - 1)
        if k < PASSES - 1:
            pack_columns(k + 1)
            send_halos(k + 1)

    out_copy = pltpu.make_async_copy(result, shrunk_hbm, out_sems.at[0])
    out_copy.start()

    def move(d):
        there = lax.rem(z + d, nz)
        rows = pl.ds(pl.multiple_of(there * own, 8), own)
        return pltpu.make_async_remote_copy(
            src_ref=anchor.at[:, rows, :], dst_ref=owned.at[pl.ds(z * F, F)],
            send_sem=move_send.at[d], recv_sem=move_recv.at[d],
            device_id=(r, c, there), device_id_type=MESH,
        )

    def take(d):
        source = lax.rem(z - d + nz, nz)
        rows = pl.ds(pl.multiple_of(z * own, 8), own)
        return pltpu.make_async_remote_copy(
            src_ref=anchor.at[:, rows, :], dst_ref=owned.at[pl.ds(source * F, F)],
            send_sem=move_send.at[d], recv_sem=move_recv.at[d],
            device_id=(r, c, source), device_id_type=MESH,
        )

    for d in range(1, nz):
        move(d).start()
    my_rows = pl.ds(pl.multiple_of(z * own, 8), own)
    keep = pltpu.make_async_copy(
        anchor.at[:, my_rows, :], owned.at[pl.ds(z * F, F)], small_sem.at[0]
    )
    keep.start()

    def store_cross(i, j, value):
        sums[rank + j, i : i + 1, :] = value

    for i in range(0, rank, 4):
        products(basis, anchor, range(i, i + 4), range(F), store_cross)

    lane_r = lax.broadcasted_iota(jnp.int32, (rank, 128), 1)
    row_r = lax.broadcasted_iota(jnp.int32, (rank, 128), 0)
    part = jnp.zeros((rank, 128), jnp.float32)
    for q in range(rank + F):
        part = jnp.where(lane_r == q, jnp.sum(sums[q], axis=1, keepdims=True), part)
    group = nr * nc
    me = r * nc + c
    parts[me] = part

    def share_part(d):
        other = lax.rem(me + d, group)
        return pltpu.make_async_remote_copy(
            src_ref=parts.at[me], dst_ref=parts.at[me],
            send_sem=part_send.at[d], recv_sem=part_recv.at[d],
            device_id=(other // nc, lax.rem(other, nc), z), device_id_type=MESH,
        )

    def take_part(d):
        other = lax.rem(me - d + group, group)
        return pltpu.make_async_remote_copy(
            src_ref=parts.at[me], dst_ref=parts.at[other],
            send_sem=part_send.at[d], recv_sem=part_recv.at[d],
            device_id=(other // nc, lax.rem(other, nc), z), device_id_type=MESH,
        )

    for d in range(1, group):
        share_part(d).start()
    for d in range(1, group):
        take_part(d).wait_recv()
    total = parts[0]
    for i in range(1, group):
        total = total + parts[i]
    pixel_ridge = ridge_share * H * W * group
    diagonal = lane_r == row_r
    before = jnp.zeros((rank, 128), jnp.float32)
    for q in range(rank):
        for f in range(F):
            before = jnp.where((row_r == q) & (lane_r == rank + f), coeff_ref[f, q], before)
    total = total + pixel_ridge * (jnp.where(diagonal, 1.0, 0.0) + before)
    solved = eliminate(total, rank)
    shares[z] = solved
    rows_out[...] = solved

    def share_rows(d):
        return pltpu.make_async_remote_copy(
            src_ref=shares.at[z], dst_ref=shares.at[z],
            send_sem=share_send.at[d], recv_sem=share_recv.at[d],
            device_id=(r, c, lax.rem(z + d, nz)), device_id_type=MESH,
        )

    def take_rows(d):
        source = lax.rem(z - d + nz, nz)
        return pltpu.make_async_remote_copy(
            src_ref=shares.at[z], dst_ref=shares.at[source],
            send_sem=share_send.at[d], recv_sem=share_recv.at[d],
            device_id=(r, c, source), device_id_type=MESH,
        )

    for d in range(1, nz):
        share_rows(d).start()
    for d in range(1, nz):
        take_rows(d).wait_recv()
    frames = F * nz
    wide = jnp.zeros((rank, 128), jnp.float32)
    for i in range(nz):
        placed = shares[i] if i == 0 else pltpu.roll(shares[i], i * F, 1)
        wide = jnp.where(
            (lane_r >= rank + i * F) & (lane_r < rank + (i + 1) * F), placed, wide
        )
    square[...] = jnp.zeros_like(square)
    square[0:rank, :] = wide
    gram = lax.dot_general(
        wide, square[...], (((1,), (1,)), ((), ())),
        precision=lax.Precision.HIGHEST, preferred_element_type=jnp.float32,
    )
    frame_ridge = ridge_share * frames
    system = jnp.where(diagonal, gram + frame_ridge, gram) + wide
    system = system + jnp.where(lane_r == row_r + rank + frames, frame_ridge, 0.0)
    table[...] = eliminate(system, rank)
    to_scalar = pltpu.make_async_copy(table, table_smem, small_sem.at[1])
    to_scalar.start()
    to_scalar.wait()
    keep.wait()
    for d in range(1, nz):
        take(d).wait_recv()

    @pl.loop(0, own // 8)
    def _(step):
        rows = pl.ds(pl.multiple_of(step * 8, 8), 8)
        old = pl.ds(pl.multiple_of(z * own + step * 8, 8), 8)

        for half in range(0, rank, 8):
            totals = [None] * 8
            for f in range(frames + rank):
                plane = owned[f, rows, :] if f < frames else basis[f - frames, old, :]
                for q in range(8):
                    term = table_smem[half + q, rank + f] * plane
                    totals[q] = term if totals[q] is None else totals[q] + term
            for q in range(8):
                target_rows = totals[q]
                barrier_own[half + q, rows, :] = target_rows

    last_copy = pltpu.make_async_copy(barrier_own, new_basis_hbm, out_sems.at[1])
    last_copy.start()
    for k in range(PASSES):
        finish_sends(k)
    for d in range(1, nz):
        move(d).wait_send()
        share_rows(d).wait_send()
    for d in range(1, group):
        share_part(d).wait_send()
    out_copy.wait()
    last_copy.wait()


def whole_kernel(video, multiplier, foreground, basis, coefficients):
    F, H, W = video.shape
    rank = basis.shape[0]
    nr, nc, nz = (lax.axis_size(name) for name in ("row", "col", "frame"))
    f32 = jnp.float32
    own = H // nz
    group = nr * nc
    vmem = pltpu.VMEM
    dma = pltpu.SemaphoreType.DMA
    shrunk, rows, new_basis = pl.pallas_call(
        functools.partial(kernel, (F, H, W, rank, nr, nc, nz)),
        out_shape=(
            jax.ShapeDtypeStruct((F, H, W), f32),
            jax.ShapeDtypeStruct((rank, 128), f32),
            jax.ShapeDtypeStruct((rank, own, W), f32),
        ),
        in_specs=[pl.BlockSpec(memory_space=pltpu.SMEM)]
        + [pl.BlockSpec(memory_space=pl.ANY)] * 4,
        out_specs=(
            pl.BlockSpec(memory_space=pl.ANY),
            pl.BlockSpec(memory_space=pltpu.VMEM),
            pl.BlockSpec(memory_space=pl.ANY),
        ),
        scratch_shapes=[
            vmem((PASSES, F + 2, H + 16, W), f32),
            vmem((F, H, W), f32),
            vmem((F, H, W), f32),
            vmem((rank, H, W), f32),
            vmem((F, H, W), f32),
            vmem((F, H, W), f32),
            vmem((F, H, W), f32),
            vmem((F * nz, own, W), f32),
            vmem((PASSES, 2, 8, H), f32),
            vmem((PASSES, 4, 8, H), f32),
            vmem((PASSES, 2, F, 8, 128), f32),
            vmem((H + 16, 128), f32),
            vmem((H, 128), f32),
            vmem((H, 128), f32),
            vmem((rank + F, rank, 128), f32),
            vmem((group, rank, 128), f32),
            vmem((nz, rank, 128), f32),
            vmem((128, 128), f32),
            vmem((rank, 128), f32),
            pltpu.SMEM((rank, 128), f32),
            dma((4,)),
            dma((2,)),
            dma((PASSES, 12)),
            dma((PASSES, 12)),
            dma((group,)),
            dma((group,)),
            dma((nz,)),
            dma((nz,)),
            dma((nz,)),
            dma((nz,)),
            dma((2,)),
            vmem((rank, own, W), f32),
        ],
        compiler_params=pltpu.CompilerParams(
            collective_id=0, has_side_effects=True, vmem_limit_bytes=60 * 1024 * 1024
        ),
    )(coefficients, video, multiplier, foreground, basis)
    return (shrunk, rows[:, rank : rank + F].T, new_basis)


def body(video, multiplier, foreground, basis, coefficients):
    F, H, W = video.shape
    rank = basis.shape[0]
    nz = lax.axis_size("frame")
    fits = (
        H % nz == 0 and (H // nz) % 8 == 0 and H % CHUNK == 0 and W % 128 == 0
        and F <= 8 and rank % 8 == 0 and 2 * rank + F * nz <= 128
    )
    run = whole_kernel if fits else local
    return run(video, multiplier, foreground, basis, coefficients)


def solution(mesh):
    placed = (
        P("frame", "row", "col"),
        P("frame", "row", "col"),
        P("frame", "row", "col"),
        P(None, "row", "col"),
        P("frame", None),
    )
    return jax.shard_map(
        body,
        mesh=mesh,
        in_specs=placed,
        out_specs=(P("frame", "row", "col"), P("frame", None), P(None, ("row", "frame"), "col")),
        check_vma=False,
    )
```

```python
import functools

import jax
import jax.numpy as jnp
from jax import lax
from jax.experimental import pallas as pl
from jax.experimental.pallas import tpu as pltpu
from jax.sharding import PartitionSpec as P

PASSES = 3


relax_rate = 0.8
smooth_weight = 0.5
smooth_floor = 0.25
shrink_level = 0.4
dual_scale = 0.8
ridge_share = 0.1


def with_halo(block, sides, width):
    for axis, dim in sides:
        count = lax.axis_size(axis)
        forward = [(i, i + 1) for i in range(count - 1)]
        backward = [(target, source) for source, target in forward]
        low = lax.ppermute(
            lax.slice_in_dim(block, block.shape[dim] - width, None, axis=dim), axis, forward
        )
        high = lax.ppermute(lax.slice_in_dim(block, 0, width, axis=dim), axis, backward)
        block = jnp.concatenate([low, block, high], axis=dim)
    return block


def forward_cells(padded, direction, shape):
    starts = [0, 0, 0]
    starts[direction] = 1
    limits = [starts[axis_dim] + shape[axis_dim] for axis_dim in range(3)]
    return lax.slice(padded, starts, limits)


def descend(padded, source, anchor, extent):
    shape = tuple((int(length) - 1 for length in padded.shape))
    here_cells = padded[:-1, :-1, :-1]
    slopes = []
    for direction in range(3):
        ahead_cells = forward_cells(padded, direction, shape)
        places = anchor[direction] + jnp.arange(shape[direction], dtype=jnp.int32)
        inside = (places >= 0) & (places < extent[direction] - 1)
        layout = [1, 1, 1]
        layout[direction] = shape[direction]
        inside = inside.reshape(layout)
        slopes.append(jnp.where(inside, ahead_cells - here_cells, jnp.zeros_like(here_cells)))
    weight = lax.rsqrt(
        smooth_floor + slopes[0] * slopes[0] + slopes[1] * slopes[1] + slopes[2] * slopes[2]
    )
    fluxes = [slope_part * weight for slope_part in slopes]
    spread = (
        fluxes[0][1:, 1:, 1:]
        - fluxes[0][:-1, 1:, 1:]
        + (fluxes[1][1:, 1:, 1:] - fluxes[1][1:, :-1, 1:])
        + (fluxes[2][1:, 1:, 1:] - fluxes[2][1:, 1:, :-1])
    )
    center = padded[1:-1, 1:-1, 1:-1]
    return center + relax_rate * (source - center + smooth_weight * spread)


def solve_definite(matrix, right_side):
    factor_lower = jnp.linalg.cholesky(matrix)
    half_solved = lax.linalg.triangular_solve(factor_lower, right_side, left_side=True, lower=True)
    return lax.linalg.triangular_solve(
        factor_lower, half_solved, left_side=True, lower=True, transpose_a=True
    )


def local(video, multiplier, foreground, basis, coefficients):
    highest = lax.Precision.HIGHEST
    frames_here, rows_here, cols_here = video.shape
    rank_size = basis.shape[0]
    frame_count = lax.axis_size("frame")
    row_count = lax.axis_size("row")
    col_count = lax.axis_size("col")
    extent = (frames_here * frame_count, rows_here * row_count, cols_here * col_count)
    frame_slot = lax.axis_index("frame")
    corner = (
        frame_slot * frames_here,
        lax.axis_index("row") * rows_here,
        lax.axis_index("col") * cols_here,
    )
    pixels = rows_here * cols_here
    flat_basis = basis.reshape(rank_size, pixels)
    background = jnp.dot(coefficients, flat_basis, precision=highest).reshape(video.shape)
    target = video - background + dual_scale * multiplier
    current = foreground
    for sweep in range(PASSES):
        padded = with_halo(current, (("row", 1), ("col", 2), ("frame", 0)), 1)
        current = descend(padded, target, tuple((start_cell - 1 for start_cell in corner)), extent)
    shrunk = current - jnp.clip(current, -shrink_level, shrink_level)
    residual_target = video + dual_scale * multiplier - shrunk
    flat_target = residual_target.reshape(frames_here, pixels)
    gram_part = jnp.dot(flat_basis, flat_basis.T, precision=highest)
    cross_part = jnp.dot(flat_basis, flat_target.T, precision=highest)
    gram_sum, cross_sum = lax.psum((gram_part, cross_part), ("row", "col"))
    identity_matrix = jnp.eye(rank_size, dtype=gram_sum.dtype)
    pixel_ridge = ridge_share * pixels * row_count * col_count
    coeff_rows = solve_definite(
        gram_sum + pixel_ridge * identity_matrix, cross_sum + pixel_ridge * coefficients.T
    )
    total_part = jnp.dot(coeff_rows, flat_target, precision=highest).reshape(
        rank_size, rows_here, cols_here
    )
    frame_gram_part = jnp.dot(coeff_rows, coeff_rows.T, precision=highest)
    owned_rows = rows_here // frame_count
    owned_sums = lax.psum_scatter(total_part, "frame", scatter_dimension=1, tiled=True)
    frame_gram = lax.psum(frame_gram_part, "frame")
    old_owned = lax.dynamic_slice_in_dim(basis, frame_slot * owned_rows, owned_rows, 1)
    frame_ridge = ridge_share * frames_here * frame_count
    right_side = (owned_sums + frame_ridge * old_owned).reshape(rank_size, owned_rows * cols_here)
    new_basis = solve_definite(frame_gram + frame_ridge * identity_matrix, right_side)
    return (shrunk, coeff_rows.T, new_basis.reshape(rank_size, owned_rows, cols_here))


MESH = pl.DeviceIdType.MESH
CHUNK = 24


def eliminate(matrix, size):
    lanes = lax.broadcasted_iota(jnp.int32, matrix.shape, 1)
    rows = lax.broadcasted_iota(jnp.int32, matrix.shape, 0)
    for k in range(size):
        pivot = matrix[k : k + 1, k : k + 1]
        scaled = matrix[k : k + 1, :] / pivot
        column = jnp.sum(jnp.where(lanes == k, matrix, 0.0), axis=1, keepdims=True)
        matrix = jnp.where(rows == k, scaled, matrix - column * scaled)
    return matrix


def kernel(
    sizes, coeff_ref, video_hbm, mult_hbm, fore_hbm, basis_hbm,
    shrunk_hbm, rows_out, new_basis_hbm,
    field, video, mult, basis, anchor, target, result, owned,
    packed, arrived, corner, edge_next, edge_flux, first_cols,
    sums, parts, shares, square, table, table_smem,
    in_sems, out_sems, halo_send, halo_recv, part_send, part_recv,
    share_send, share_recv, move_send, move_recv, small_sem, barrier_own,
):
    F, H, W, rank, nr, nc, nz = sizes
    r = lax.axis_index("row")
    c = lax.axis_index("col")
    z = lax.axis_index("frame")
    own = H // nz

    def inside(dr, dc, dz):
        ok = None
        for at, step, count in ((r, dr, nr), (c, dc, nc), (z, dz, nz)):
            if step != 0:
                test = (at + step >= 0) & (at + step < count)
                ok = test if ok is None else ok & test
        return ok

    loads = []
    for i, (src, dst) in enumerate(
        (
            (fore_hbm, field.at[0, 1 : F + 1, 8 : H + 8, :]),
            (basis_hbm, basis),
            (video_hbm, video),
            (mult_hbm, mult),
        )
    ):
        copy = pltpu.make_async_copy(src, dst, in_sems.at[i])
        copy.start()
        loads.append(copy)

    barrier = pltpu.get_barrier_semaphore()
    for d in range(1, nr * nc):
        other = lax.rem(r * nc + c + d, nr * nc)
        pl.semaphore_signal(
            barrier, inc=1, device_id=(other // nc, lax.rem(other, nc), z), device_id_type=MESH
        )
    for d in range(1, nz):
        pl.semaphore_signal(
            barrier, inc=1, device_id=(r, c, lax.rem(z + d, nz)), device_id_type=MESH
        )
    diagonals = ((1, 0, -1), (-1, 0, 1), (0, 1, -1), (0, -1, 1))
    for step in diagonals:
        @pl.when(inside(*step))
        def _(step=step):
            pl.semaphore_signal(
                barrier,
                inc=1,
                device_id=(r + step[0], c + step[1], z + step[2]),
                device_id_type=MESH,
            )
    expected = jnp.int32(nr * nc - 1 + nz - 1)
    for step in diagonals:
        expected = expected + inside(*step).astype(jnp.int32)
    pl.semaphore_wait(barrier, expected)

    lane_h = lax.broadcasted_iota(jnp.int32, (H, 128), 1)

    def pack_columns(k):
        for side in range(2):
            tile = jnp.zeros((H, 128), jnp.float32)
            for f in range(F):
                at = 0 if side == 0 else W - 1
                lanes = field[k, f + 1, 8 : H + 8, (at // 128) * 128 : (at // 128) * 128 + 128]
                column = lanes[:, at % 128 : at % 128 + 1]
                tile = jnp.where(lane_h == f, column, tile)
            if side == 0:
                first_cols[...] = tile
            packed[k, side] = tile.T[:8, :]

    def halo_list(k):
        fk = field.at[k]
        mid = slice(1, F + 1)
        return (
            (packed.at[k, 0], arrived.at[k, 0], (0, -1, 0)),
            (packed.at[k, 1], arrived.at[k, 1], (0, 1, 0)),
            (packed.at[k, 0], arrived.at[k, 2], (0, -1, 1)),
            (packed.at[k, 1], arrived.at[k, 3], (0, 1, -1)),
            (fk.at[mid, H : H + 8, :], fk.at[mid, 0:8, :], (1, 0, 0)),
            (fk.at[mid, 8:16, :], fk.at[mid, H + 8 : H + 16, :], (-1, 0, 0)),
            (fk.at[F, 8:16, :], fk.at[0, H + 8 : H + 16, :], (-1, 0, 1)),
            (fk.at[1, H : H + 8, :], fk.at[F + 1, 0:8, :], (1, 0, -1)),
            (fk.at[mid, H : H + 8, 0:128], corner.at[k, 0], (1, -1, 0)),
            (fk.at[mid, 8:16, W - 128 : W], corner.at[k, 1], (-1, 1, 0)),
        ) + tuple(
            face
            for b in range(nz)
            for rows in (slice(8 + b * own, 8 + (b + 1) * own),)
            for face in (
                (fk.at[F, rows, :], fk.at[0, rows, :], (0, 0, 1)),
                (fk.at[1, rows, :], fk.at[F + 1, rows, :], (0, 0, -1)),
            )
        )

    def halo_copy(k, i, src, dst, step):
        return pltpu.make_async_remote_copy(
            src_ref=src, dst_ref=dst,
            send_sem=halo_send.at[k, i], recv_sem=halo_recv.at[k, i],
            device_id=(r + step[0], c + step[1], z + step[2]), device_id_type=MESH,
        )

    def send_halos(k, which):
        every = halo_list(k)
        for i in which:
            src, dst, step = every[i]

            @pl.when(inside(*step))
            def _(i=i, src=src, dst=dst, step=step):
                halo_copy(k, i, src, dst, step).start()

    def wait_halos(k):
        for i, (src, dst, step) in enumerate(halo_list(k)):
            @pl.when(inside(*(-s for s in step)))
            def _(i=i, src=src, dst=dst, step=step):
                halo_copy(k, i, src, dst, step).wait_recv()

    def finish_sends(k):
        for i, (src, dst, step) in enumerate(halo_list(k)):
            @pl.when(inside(*step))
            def _(i=i, src=src, dst=dst, step=step):
                halo_copy(k, i, src, dst, step).wait_send()

    def prepare_columns(k):
        tall = jnp.concatenate([arrived[k, 0], jnp.zeros((120, H), jnp.float32)], axis=0).T
        edge = jnp.concatenate([arrived[k, 2], jnp.zeros((120, H), jnp.float32)], axis=0).T
        tile = jnp.where(lane_h == 0, edge[:, F - 1 : F], pltpu.roll(tall, 1, 1))
        edge_next[8 : H + 8, :] = tile
        lane8 = lax.broadcasted_iota(jnp.int32, (8, 128), 1)
        top = jnp.zeros((8, 128), jnp.float32)
        bottom = jnp.zeros((1, 128), jnp.float32)
        for f in range(F):
            top = jnp.where(lane8 == f + 1, corner[k, 0, f][:, 0:1], top)
            bottom = jnp.where(lane8[:1] == f, corner[k, 1, f][0:1, 127:128], bottom)
        edge_next[0:8, :] = top
        edge_next[H + 8 : H + 16, :] = jnp.zeros((8, 128), jnp.float32)
        here = jnp.concatenate([arrived[k, 1], jnp.zeros((120, H), jnp.float32)], axis=0).T
        edge = jnp.concatenate([arrived[k, 3], jnp.zeros((120, H), jnp.float32)], axis=0).T
        ahead = jnp.where(lane_h == F - 1, edge[:, 0:1], pltpu.roll(here, 127, 1))
        slope0 = jnp.where((lane_h == F - 1) & (z == nz - 1), 0.0, ahead - here)
        row_h = lax.broadcasted_iota(jnp.int32, (H, 128), 0)
        below = jnp.where(row_h == H - 1, bottom, pltpu.roll(here, H - 1, 0))
        slope1 = jnp.where((row_h == H - 1) & (r == nr - 1), 0.0, below - here)
        slope2 = first_cols[...] - here
        weight = lax.rsqrt(smooth_floor + slope0 * slope0 + slope1 * slope1 + slope2 * slope2)
        edge_flux[...] = jnp.where(c == 0, 0.0, slope2 * weight)

    def sweep(k, last, base):
        @pl.loop(0, own // CHUNK)
        def _(step):
            start = pl.multiple_of(base + step * CHUNK, 8)
            R = CHUNK
            lane_t = lax.broadcasted_iota(jnp.int32, (R + 8, 128), 1)
            row_t = lax.broadcasted_iota(jnp.int32, (R + 8, W), 0) + (r * H + start - 8)
            lane_w = lax.broadcasted_iota(jnp.int32, (R + 8, W), 1)
            blocked = (row_t < 0) | (row_t >= nr * H - 1)
            columns = edge_next[pl.ds(start, R + 8), :]
            fluxes_in = edge_flux[pl.ds(start, R), :]
            now = field[k, 0, pl.ds(start, R + 16), :]
            flux0_before = None
            for f in range(-1, F):
                after = field[k, f + 2, pl.ds(start, R + 16), :]
                here = now[: R + 8]
                below = pltpu.roll(now, R + 15, 0)[: R + 8]
                ahead = after[: R + 8]
                wall = columns[:, f + 1 : f + 2]
                beyond = jnp.where(c == nc - 1, here, jnp.broadcast_to(wall, here.shape))
                right = jnp.where(lane_w == W - 1, beyond, pltpu.roll(here, W - 1, 1))
                slope0 = ahead - here
                if f == F - 1:
                    slope0 = jnp.where(z == nz - 1, 0.0, slope0)
                slope1 = jnp.where(blocked, 0.0, below - here)
                slope2 = right - here
                weight = lax.rsqrt(
                    smooth_floor + slope0 * slope0 + slope1 * slope1 + slope2 * slope2
                )
                flux0 = (slope0 * weight)[8:]
                if f < 0:
                    flux0 = jnp.where(z == 0, 0.0, flux0)
                else:
                    flux1 = jnp.where(row_t < 0, 0.0, slope1 * weight)
                    flux2 = (slope2 * weight)[8:]
                    above = pltpu.roll(flux1, 1, 0)[8:]
                    left = jnp.where(
                        lane_w[8:] == 0,
                        jnp.broadcast_to(fluxes_in[:, f : f + 1], flux2.shape),
                        pltpu.roll(flux2, 1, 1),
                    )
                    spread = flux0 - flux0_before + (flux1[8:] - above) + (flux2 - left)
                    center = here[8:]
                    at = pl.ds(start, R)
                    value = center + relax_rate * (
                        target[f, at, :] - center + smooth_weight * spread
                    )
                    if last:
                        shrunk = value - jnp.clip(value, -shrink_level, shrink_level)
                        result[f, at, :] = shrunk
                        anchor[f, at, :] = anchor[f, at, :] - shrunk
                    else:
                        field[k + 1, f + 1, pl.ds(start + 8, R), :] = value
                flux0_before = flux0
                now = after

    def products(left_of, right_of, lefts, rights, store):
        zero = jnp.zeros((8, 128), jnp.float32)

        def body(step, totals):
            rows = pl.ds(pl.multiple_of(step * 8, 8), 8)
            a = [left_of[i, rows, :] for i in lefts]
            b = [right_of[j, rows, :] for j in rights]
            out = []
            for x in range(len(lefts)):
                for y in range(len(rights)):
                    prod = a[x] * b[y]
                    total = totals[len(out)]
                    for w in range(W // 128):
                        total = total + prod[:, w * 128 : w * 128 + 128]
                    out.append(total)
            return tuple(out)

        totals = lax.fori_loop(0, H // 8, body, (zero,) * (len(lefts) * len(rights)), unroll=2)
        n = 0
        for i in lefts:
            for j in rights:
                store(i, j, jnp.sum(totals[n], axis=0, keepdims=True))
                n += 1

    loads[0].wait()
    send_halos(0, range(10, 10 + 2 * nz))
    send_halos(0, range(4, 10))
    pack_columns(0)
    send_halos(0, range(4))
    loads[1].wait()

    def store_gram(i, j, value):
        sums[j, i : i + 1, :] = value
        if i // 4 != j // 4:
            sums[i, j : j + 1, :] = value

    for i in range(0, rank, 4):
        for j in range(i, rank, 4):
            products(basis, basis, range(i, i + 4), range(j, j + 4), store_gram)

    loads[2].wait()
    loads[3].wait()

    @pl.loop(0, H // 8)
    def _(step):
        rows = pl.ds(pl.multiple_of(step * 8, 8), 8)
        totals = [None] * F
        for q in range(rank):
            plane = basis[q, rows, :]
            for f in range(F):
                term = coeff_ref[f, q] * plane
                totals[f] = term if totals[f] is None else totals[f] + term
        for f in range(F):
            lifted = dual_scale * mult[f, rows, :]
            anchor[f, rows, :] = video[f, rows, :] + lifted
            target[f, rows, :] = video[f, rows, :] - totals[f] + lifted

    def move(d):
        there = lax.rem(z + d, nz)
        rows = pl.ds(pl.multiple_of(there * own, 8), own)
        return pltpu.make_async_remote_copy(
            src_ref=anchor.at[:, rows, :], dst_ref=owned.at[pl.ds(z * F, F)],
            send_sem=move_send.at[d], recv_sem=move_recv.at[d],
            device_id=(r, c, there), device_id_type=MESH,
        )

    def take(d):
        source = lax.rem(z - d + nz, nz)
        rows = pl.ds(pl.multiple_of(z * own, 8), own)
        return pltpu.make_async_remote_copy(
            src_ref=anchor.at[:, rows, :], dst_ref=owned.at[pl.ds(source * F, F)],
            send_sem=move_send.at[d], recv_sem=move_recv.at[d],
            device_id=(r, c, source), device_id_type=MESH,
        )

    for k in range(PASSES):
        wait_halos(k)
        prepare_columns(k)
        if k < PASSES - 1:
            for b in range(nz):
                sweep(k, False, b * own)
                send_halos(k + 1, (10 + 2 * b, 11 + 2 * b))
            send_halos(k + 1, range(4, 10))
            pack_columns(k + 1)
            send_halos(k + 1, range(4))
        else:
            for d in range(1, nz + 1):
                sweep(k, True, lax.rem(z + d, nz) * own)
                if d < nz:
                    move(d).start()

    out_copy = pltpu.make_async_copy(result, shrunk_hbm, out_sems.at[0])
    out_copy.start()

    my_rows = pl.ds(pl.multiple_of(z * own, 8), own)
    keep = pltpu.make_async_copy(
        anchor.at[:, my_rows, :], owned.at[pl.ds(z * F, F)], small_sem.at[0]
    )
    keep.start()

    def store_cross(i, j, value):
        sums[rank + j, i : i + 1, :] = value

    for i in range(0, rank, 4):
        products(basis, anchor, range(i, i + 4), range(F), store_cross)

    lane_r = lax.broadcasted_iota(jnp.int32, (rank, 128), 1)
    row_r = lax.broadcasted_iota(jnp.int32, (rank, 128), 0)
    part = jnp.zeros((rank, 128), jnp.float32)
    for q in range(rank + F):
        part = jnp.where(lane_r == q, jnp.sum(sums[q], axis=1, keepdims=True), part)
    group = nr * nc
    me = r * nc + c
    parts[me] = part

    def share_part(d):
        other = lax.rem(me + d, group)
        return pltpu.make_async_remote_copy(
            src_ref=parts.at[me], dst_ref=parts.at[me],
            send_sem=part_send.at[d], recv_sem=part_recv.at[d],
            device_id=(other // nc, lax.rem(other, nc), z), device_id_type=MESH,
        )

    def take_part(d):
        other = lax.rem(me - d + group, group)
        return pltpu.make_async_remote_copy(
            src_ref=parts.at[me], dst_ref=parts.at[other],
            send_sem=part_send.at[d], recv_sem=part_recv.at[d],
            device_id=(other // nc, lax.rem(other, nc), z), device_id_type=MESH,
        )

    for d in range(1, group):
        share_part(d).start()
    for d in range(1, group):
        take_part(d).wait_recv()
    total = parts[0]
    for i in range(1, group):
        total = total + parts[i]
    pixel_ridge = ridge_share * H * W * group
    diagonal = lane_r == row_r
    before = jnp.zeros((rank, 128), jnp.float32)
    for q in range(rank):
        for f in range(F):
            before = jnp.where((row_r == q) & (lane_r == rank + f), coeff_ref[f, q], before)
    total = total + pixel_ridge * (jnp.where(diagonal, 1.0, 0.0) + before)
    solved = eliminate(total, rank)
    shares[z] = solved
    rows_out[...] = solved

    def share_rows(d):
        return pltpu.make_async_remote_copy(
            src_ref=shares.at[z], dst_ref=shares.at[z],
            send_sem=share_send.at[d], recv_sem=share_recv.at[d],
            device_id=(r, c, lax.rem(z + d, nz)), device_id_type=MESH,
        )

    def take_rows(d):
        source = lax.rem(z - d + nz, nz)
        return pltpu.make_async_remote_copy(
            src_ref=shares.at[z], dst_ref=shares.at[source],
            send_sem=share_send.at[d], recv_sem=share_recv.at[d],
            device_id=(r, c, source), device_id_type=MESH,
        )

    for d in range(1, nz):
        share_rows(d).start()
    for d in range(1, nz):
        take_rows(d).wait_recv()
    frames = F * nz
    wide = jnp.zeros((rank, 128), jnp.float32)
    for i in range(nz):
        placed = shares[i] if i == 0 else pltpu.roll(shares[i], i * F, 1)
        wide = jnp.where(
            (lane_r >= rank + i * F) & (lane_r < rank + (i + 1) * F), placed, wide
        )
    square[...] = jnp.zeros_like(square)
    square[0:rank, :] = wide
    gram = lax.dot_general(
        wide, square[...], (((1,), (1,)), ((), ())),
        precision=lax.Precision.HIGHEST, preferred_element_type=jnp.float32,
    )
    frame_ridge = ridge_share * frames
    system = jnp.where(diagonal, gram + frame_ridge, gram) + wide
    system = system + jnp.where(lane_r == row_r + rank + frames, frame_ridge, 0.0)
    table[...] = eliminate(system, rank)
    to_scalar = pltpu.make_async_copy(table, table_smem, small_sem.at[1])
    to_scalar.start()
    to_scalar.wait()
    keep.wait()
    for d in range(1, nz):
        take(d).wait_recv()

    @pl.loop(0, own // 8)
    def _(step):
        rows = pl.ds(pl.multiple_of(step * 8, 8), 8)
        old = pl.ds(pl.multiple_of(z * own + step * 8, 8), 8)

        for half in range(0, rank, 8):
            totals = [None] * 8
            for f in range(frames + rank):
                plane = owned[f, rows, :] if f < frames else basis[f - frames, old, :]
                for q in range(8):
                    term = table_smem[half + q, rank + f] * plane
                    totals[q] = term if totals[q] is None else totals[q] + term
            for q in range(8):
                target_rows = totals[q]
                barrier_own[half + q, rows, :] = target_rows

    last_copy = pltpu.make_async_copy(barrier_own, new_basis_hbm, out_sems.at[1])
    last_copy.start()
    for k in range(PASSES):
        finish_sends(k)
    for d in range(1, nz):
        move(d).wait_send()
        share_rows(d).wait_send()
    for d in range(1, group):
        share_part(d).wait_send()
    out_copy.wait()
    last_copy.wait()


def whole_kernel(video, multiplier, foreground, basis, coefficients):
    F, H, W = video.shape
    rank = basis.shape[0]
    nr, nc, nz = (lax.axis_size(name) for name in ("row", "col", "frame"))
    f32 = jnp.float32
    own = H // nz
    group = nr * nc
    vmem = pltpu.VMEM
    dma = pltpu.SemaphoreType.DMA
    shrunk, rows, new_basis = pl.pallas_call(
        functools.partial(kernel, (F, H, W, rank, nr, nc, nz)),
        out_shape=(
            jax.ShapeDtypeStruct((F, H, W), f32),
            jax.ShapeDtypeStruct((rank, 128), f32),
            jax.ShapeDtypeStruct((rank, own, W), f32),
        ),
        in_specs=[pl.BlockSpec(memory_space=pltpu.SMEM)]
        + [pl.BlockSpec(memory_space=pl.ANY)] * 4,
        out_specs=(
            pl.BlockSpec(memory_space=pl.ANY),
            pl.BlockSpec(memory_space=pltpu.VMEM),
            pl.BlockSpec(memory_space=pl.ANY),
        ),
        scratch_shapes=[
            vmem((PASSES, F + 2, H + 16, W), f32),
            vmem((F, H, W), f32),
            vmem((F, H, W), f32),
            vmem((rank, H, W), f32),
            vmem((F, H, W), f32),
            vmem((F, H, W), f32),
            vmem((F, H, W), f32),
            vmem((F * nz, own, W), f32),
            vmem((PASSES, 2, 8, H), f32),
            vmem((PASSES, 4, 8, H), f32),
            vmem((PASSES, 2, F, 8, 128), f32),
            vmem((H + 16, 128), f32),
            vmem((H, 128), f32),
            vmem((H, 128), f32),
            vmem((rank + F, rank, 128), f32),
            vmem((group, rank, 128), f32),
            vmem((nz, rank, 128), f32),
            vmem((128, 128), f32),
            vmem((rank, 128), f32),
            pltpu.SMEM((rank, 128), f32),
            dma((4,)),
            dma((2,)),
            dma((PASSES, 10 + 2 * nz)),
            dma((PASSES, 10 + 2 * nz)),
            dma((group,)),
            dma((group,)),
            dma((nz,)),
            dma((nz,)),
            dma((nz,)),
            dma((nz,)),
            dma((2,)),
            vmem((rank, own, W), f32),
        ],
        compiler_params=pltpu.CompilerParams(
            collective_id=0, has_side_effects=True, vmem_limit_bytes=60 * 1024 * 1024
        ),
    )(coefficients, video, multiplier, foreground, basis)
    return (shrunk, rows[:, rank : rank + F].T, new_basis)


def body(video, multiplier, foreground, basis, coefficients):
    F, H, W = video.shape
    rank = basis.shape[0]
    nz = lax.axis_size("frame")
    fits = (
        H % nz == 0 and (H // nz) % 8 == 0 and (H // nz) % CHUNK == 0 and W % 128 == 0
        and F <= 8 and rank % 8 == 0 and 2 * rank + F * nz <= 128
    )
    run = whole_kernel if fits else local
    return run(video, multiplier, foreground, basis, coefficients)


def solution(mesh):
    placed = (
        P("frame", "row", "col"),
        P("frame", "row", "col"),
        P("frame", "row", "col"),
        P(None, "row", "col"),
        P("frame", None),
    )
    return jax.shard_map(
        body,
        mesh=mesh,
        in_specs=placed,
        out_specs=(P("frame", "row", "col"), P("frame", None), P(None, ("row", "frame"), "col")),
        check_vma=False,
    )
```
